32 devices in a mesh: slab: 8 (over y, x, core), tile: 4 (over z).
Axes of the slice: x: 2, y: 2, z: 4, core: 2. Of those that a mesh axis runs over, the one named last changes fastest.
Arguments:
- particle_features: bfloat16 [6, 131072], P(None, ('slab', 'tile')), may hold values from -6 to 6
- destination: int32 [131072, 1], P(('slab', 'tile')), may hold values from 0 to 7; in each aligned block of 4096 rows (0 to 4095, 4096 to 8191, ...) at most 2048 rows name the same one
- cell_index: int32 [131072], P(('slab', 'tile')), may hold values from 0 to 16383
- offset_code: int32 [131072], P(('slab', 'tile')), may hold values from 0 to 262143
- live_count: int32 [32], P(('slab', 'tile')), may hold values from 2048 to 4096, as said below
- lift_weight: bfloat16 [3, 3, 64, 18], replicated, may hold values from -0.5 to 0.5
- fine_weight: bfloat16 [3, 3, 64, 192], replicated, may hold values from -0.15625 to 0.15625
- down_weight: bfloat16 [2, 2, 2, 256, 64], replicated, may hold values from -0.25 to 0.25
- coarse_weight: bfloat16 [3, 3, 256, 768], replicated, may hold values from -0.078125 to 0.078125
- up_weight: bfloat16 [2, 2, 2, 64, 256], replicated, may hold values from -0.375 to 0.375
- merge_weight: bfloat16 [3, 3, 64, 192], replicated, may hold values from -0.15625 to 0.15625
- head_weight: bfloat16 [3, 64], replicated, may hold values from -0.75 to 0.75
Outputs:
- displacement: float32 [3, 32, 32, 128], P(None, 'slab', 'tile')
The draws below stay inside these ranges and needn't reach their ends.
Inputs may be any that keep to these rules, and one draw needn't show every extreme that they name: `destination`: among the rows of one device, at most 2048 name the same slab; some slab is named by exactly 2048 of them. `live_count`: some device has all 4096 rows live.
All inputs are finite; a program needn't handle non-finite values.
Results may differ from the reference program's by a relative error of at most 0.024.
Values may be sent and summed in bfloat16 or wider, within the bound.
A program may use at most 192 MiB of HBM per device.

```python
import math
import jax
import jax.numpy as jnp
import numpy as np
from jax import lax

ATTR = 6
C0 = 64
C1 = 256
C_OUT = 3
NX = 128
CZ = 4
NDEV = 32
NY = 32
NZ = 32
P_DEV = 4096
CAP = 2048
PARTICLES = 131072
N_SLAB = 8


def draw_live_count(key, part):
    first_key, second_key = jax.random.split(jax.random.fold_in(key, 17))
    counts = jax.random.randint(first_key, (NDEV,), P_DEV // 2, P_DEV + 1)
    chosen = jax.random.randint(second_key, (), 0, NDEV)
    return jnp.where(jnp.arange(NDEV) == chosen, P_DEV, counts).astype(jnp.int32)


def touch_ends(result, rng, least, top_value):
    index_at = [jax.random.randint(jax.random.fold_in(rng, axis), (), 0, length) for axis, length in enumerate(result.shape)]
    main_axis = result.shape.index(max(result.shape))
    next_to = index_at[:main_axis] + [(index_at[main_axis] + 1) % result.shape[main_axis]] + index_at[main_axis + 1:]
    return result.at[tuple(index_at)].set(least).at[tuple(next_to)].set(top_value)


def steps_of(key, shape, pieces, low, high):
    def one(dim, blocks):
        draws = jax.random.uniform(jax.random.fold_in(jax.random.fold_in(key, 6), dim), (blocks,), jnp.float32, low / len(pieces), high / len(pieces))
        return jnp.repeat(jnp.exp(draws), shape[dim] // blocks).reshape((-1,) + (1,) * (len(shape) - dim - 1))

    factor_of = one(*pieces[0])
    for cut in pieces[1:]:
        factor_of = factor_of * one(*cut)
    return factor_of


def deal_out(own_key, own, number, rows, number_of, top, bound, skew):
    ranking = jax.random.permutation(own_key, number_of)
    crowded, usual = shares(number_of, rows * top, bound, skew, True), shares(number_of, rows * top, bound, skew, False)
    places = jnp.arange(number_of)

    def named(sizes, offset_by):
        used = int((sizes > 0).sum())
        fixed = max(1, used // 4)
        passed = fixed + (places - fixed + offset_by * (used - fixed)) % max(1, number_of - fixed)
        return jnp.zeros((number_of,), jnp.int32).at[ranking[jnp.where(places < fixed, places, passed)]].set(jnp.asarray(sizes, jnp.int32))

    sizes = jnp.where(number % 4 == 0, named(crowded, number // 4), named(usual, number - number // 4 - 1))
    mixed = jax.random.permutation(jax.random.fold_in(own, 3), number_of)
    donor, taker = mixed[0:number_of // 2 * 2:2], mixed[1:number_of // 2 * 2:2]
    slack = jnp.minimum(sizes[donor] - 1, bound - sizes[taker]) // 2
    slack = jnp.where((donor == ranking[0]) | (taker == ranking[0]) | (sizes[taker] == 0), 0, jnp.maximum(slack, 0))
    passed = jax.random.randint(jax.random.fold_in(own, 4), (number_of // 2,), 0, 1 << 20) % (slack + 1)
    sizes = sizes.at[donor].add(-passed).at[taker].add(passed)
    items = jnp.searchsorted(jnp.cumsum(sizes), jnp.arange(rows * top), side="right").astype(jnp.int32)
    table = items.reshape(top, rows).T
    table = table[jax.random.permutation(jax.random.fold_in(own, 1), rows)]
    offset_by = jax.random.randint(jax.random.fold_in(own, 2), (rows, 1), 0, top)
    return jnp.take_along_axis(table, (jnp.arange(top)[None, :] + offset_by) % top, axis=1)


def shares(count, total, reach, skew, full):
    portions = [(1 << 20) // math.isqrt(standing ** skew) + 1 for standing in range(1, count + 1)]
    largest = reach if full else min(reach, max(-(-total // count), total * portions[0] // sum(portions)))
    least = 1 if total - largest >= count - 1 else 0
    given, rest = [largest] + [least] * (count - 1), total - largest - least * (count - 1)
    while rest > 0:
        candidates = [i for i in range(1, count) if given[i] < largest] or [i for i in range(1, count) if given[i] < reach]
        whole, remaining = sum([portions[i] for i in candidates]), rest
        for i in candidates:
            extra = min(reach - given[i], max(1, remaining * portions[i] // whole), rest)
            given[i] = given[i] + extra
            rest = rest - extra
    return np.array(given)


def noise(key, shape, deviation, most, cuts=(), kind=jnp.bfloat16):
    factor_of = steps_of(key, shape, cuts, -0.22, 0.18) if cuts else 1.0
    array = jax.random.normal(key, shape, jnp.float32) * deviation * factor_of
    return jnp.minimum(jnp.maximum(array, -most), most).astype(kind)


def setup_inputs(seed: int = 0) -> dict:
    seeds = jax.random.split(jax.random.key(seed), 13)
    particle_features = noise(seeds[0], (ATTR, PARTICLES), 1.0, 6.0, ((1, 32),))
    destination_keys = jax.random.split(jax.random.fold_in(seeds[1], 1), PARTICLES // P_DEV)
    destination_turns = jax.random.permutation(jax.random.fold_in(seeds[1], 3), PARTICLES // P_DEV)
    destination = jax.vmap(lambda own, number: deal_out(jax.random.fold_in(seeds[1], 2), own, number, P_DEV, N_SLAB, 1, CAP, 2))(destination_keys, destination_turns).reshape((PARTICLES, 1))
    cell_index = touch_ends(jax.random.randint(seeds[2], (PARTICLES,), 0, CZ * NY * NX), jax.random.fold_in(seeds[2], 1), 0, (CZ * NY * NX) - 1).astype(jnp.int32)
    offset_code = touch_ends(jax.random.randint(seeds[3], (PARTICLES,), 0, 262144), jax.random.fold_in(seeds[3], 1), 0, 262143).astype(jnp.int32)
    live_count = draw_live_count(jax.random.fold_in(seeds[12], 71), 0)
    lift_weight = noise(seeds[5], (3, 3, C0, 3 * ATTR), (27 * ATTR) ** -0.5, 0.5)
    fine_weight = noise(seeds[6], (3, 3, C0, 3 * C0), (27 * C0) ** -0.5, 0.15625)
    down_weight = noise(seeds[7], (2, 2, 2, C1, C0), (8 * C0) ** -0.5, 0.25)
    coarse_weight = noise(seeds[8], (3, 3, C1, 3 * C1), (27 * C1) ** -0.5, 0.078125)
    up_weight = noise(seeds[9], (2, 2, 2, C0, C1), C1 ** -0.5, 0.375)
    merge_weight = noise(seeds[10], (3, 3, C0, 3 * C0), (27 * C0) ** -0.5, 0.15625)
    head_weight = noise(seeds[11], (C_OUT, C0), C0 ** -0.5, 0.75)
    return dict(particle_features=particle_features, destination=destination, cell_index=cell_index, offset_code=offset_code, live_count=live_count, lift_weight=lift_weight, fine_weight=fine_weight, down_weight=down_weight, coarse_weight=coarse_weight, up_weight=up_weight, merge_weight=merge_weight, head_weight=head_weight)


slope = 0.1


def act(values):
    return jnp.maximum(values, slope * values)


def conv_full(field, weight):
    stacked = jnp.concatenate([jnp.roll(field, 1, 3), field, jnp.roll(field, -1, 3)], 0)
    padded = jnp.concatenate([stacked[:, -1:], stacked, stacked[:, :1]], 1)
    wide = weight.astype(jnp.float32)

    def plane(index):
        block = lax.dynamic_slice_in_dim(padded, index, 3, 1).astype(jnp.float32)
        total = jnp.zeros((weight.shape[2], field.shape[2], field.shape[3]), jnp.float32)
        for a in range(3):
            for b in range(3):
                total = total + jnp.einsum('oi,iyx->oyx', wide[a, b], jnp.roll(block[:, a], 1 - b, 1))
        return total

    planes = lax.map(plane, jnp.arange(field.shape[1], dtype=jnp.int32))
    return jnp.transpose(planes, (1, 0, 2, 3))


def deposit_full(particle_features, destination, cell_index, offset_code, live_count):
    rows = jnp.arange(PARTICLES, dtype=jnp.int32)
    live = ((rows % P_DEV) < jnp.repeat(live_count, P_DEV)).astype(jnp.float32)
    values = particle_features.astype(jnp.float32) * live[None, :]
    plane_z = destination[:, 0] * CZ + cell_index // (NY * NX)
    row_y = (cell_index // NX) % NY
    col_x = cell_index % NX
    frac_z = ((offset_code // 4096) % 64).astype(jnp.float32) / 64.0
    frac_y = ((offset_code // 64) % 64).astype(jnp.float32) / 64.0
    frac_x = (offset_code % 64).astype(jnp.float32) / 64.0
    field = jnp.zeros((ATTR, NZ * NY * NX), jnp.float32)
    for a in range(2):
        for b in range(2):
            for k in range(2):
                weight_z = frac_z if a else 1.0 - frac_z
                weight_y = frac_y if b else 1.0 - frac_y
                weight_x = frac_x if k else 1.0 - frac_x
                corner = weight_z * weight_y * weight_x
                target = ((plane_z + a) % NZ) * (NY * NX) + ((row_y + b) % NY) * NX + (col_x + k) % NX
                field = field.at[:, target].add(values * corner[None, :])
    return field.reshape(ATTR, NZ, NY, NX)


def reference(particle_features, destination, cell_index, offset_code, live_count, lift_weight, fine_weight, down_weight, coarse_weight, up_weight, merge_weight, head_weight):
    grid = deposit_full(particle_features, destination, cell_index, offset_code, live_count).astype(jnp.bfloat16)
    first = act(conv_full(grid, lift_weight)).astype(jnp.bfloat16)
    second = act(conv_full(first, fine_weight)).astype(jnp.bfloat16)
    blocks = second.astype(jnp.float32).reshape(C0, NZ // 2, 2, NY // 2, 2, NX // 2, 2)
    lowered = act(jnp.einsum('abkoc,czaybxk->ozyx', down_weight.astype(jnp.float32), blocks)).astype(jnp.bfloat16)
    coarse = act(conv_full(lowered, coarse_weight)).astype(jnp.bfloat16)
    raised = jnp.einsum('abkoc,czyx->ozaybxk', up_weight.astype(jnp.float32), coarse.astype(jnp.float32)).reshape(C0, NZ, NY, NX)
    joined = (second.astype(jnp.float32) + raised).astype(jnp.bfloat16)
    merged = act(conv_full(joined, merge_weight)).astype(jnp.bfloat16)
    return jnp.einsum('oc,czyx->ozyx', head_weight.astype(jnp.float32), merged.astype(jnp.float32))
```

```python
import types

import jax
import jax.numpy as jnp
from jax import lax
from jax.experimental import pallas as pl
from jax.experimental.pallas import tpu as pltpu
from jax.sharding import PartitionSpec as P

NX = 128
YT = 8
CZ = 4
LANES = 128
UNROLLED = 4


slope = 0.1


BF16 = jnp.bfloat16
F32 = jnp.float32
MESH = pl.DeviceIdType.MESH
NT = (((1,), (1,)), ((), ()))
SIDES = [(dz, dy) for dz in (-1, 0, 1) for dy in (-1, 0, 1) if dz or dy]


def act(values):
    return jnp.maximum(values, slope * values)


def dot(left, right):
    return jnp.dot(left, right, preferred_element_type=F32)


def neighbour(dz, dy):
    slabs, tiles = lax.axis_size("slab"), lax.axis_size("tile")
    return (
        lax.rem(lax.axis_index("slab") + (dz + slabs), slabs),
        lax.rem(lax.axis_index("tile") + (dy + tiles), tiles),
    )


def flipped(mask):
    slab = lax.axis_index("slab")
    other = slab
    for b in range(mask.bit_length()):
        if mask >> b & 1:
            other = other + 2**b * (1 - 2 * (slab // 2**b % 2))
    return other, lax.axis_index("tile")


def ahead(d):
    return lax.axis_index("slab"), lax.rem(lax.axis_index("tile") + d, lax.axis_size("tile"))


def send(source, target, sems, at, device):
    copy = pltpu.make_async_remote_copy(
        src_ref=source,
        dst_ref=target,
        send_sem=sems[0].at[at],
        recv_sem=sems[1].at[at],
        device_id=device,
        device_id_type=MESH,
    )
    copy.start()
    return copy


def iota(rows, axis):
    return lax.broadcasted_iota(jnp.int32, (rows, LANES), axis)


def pack_particles(feat, dest, cell, code, live, packed, places):
    attrs = feat.shape[0]
    ny = lax.axis_size("tile") * YT
    cells, codes = cell[...], code[...]
    row = cells // NX
    high = (dest[...] * CZ + row // ny) * 64 + ((codes >> 12) & 63)
    places[0] = high * (64 * ny) + (row % ny) * 64 + ((codes >> 6) & 63)
    col = (cells % NX).astype(F32)
    frac = (codes & 63).astype(F32) * (1.0 / 64.0)
    count = cells.shape[0]
    half = count // 2
    lane = lax.broadcasted_iota(jnp.int32, (attrs, LANES), 1)
    for q in range(half):
        rows = []
        for r in (q, half + q):
            values = feat[:, r * LANES : (r + 1) * LANES].astype(F32)
            rows.append(jnp.where(lane + r * LANES < live[0], values, 0.0))
            rows.append(col[r : r + 1])
            rows.append(frac[r : r + 1])
        packed[0, :, q * LANES : (q + 1) * LANES] = jnp.concatenate(rows, 0).astype(BF16)


def place_particles(m, places, spots):
    slabs, ny = lax.axis_size("slab"), lax.axis_size("tile") * YT
    base = (lax.axis_index("slab") // 2 * (2 * CZ)).astype(F32)
    code = places[m]
    z = (code // (64 * ny)).astype(F32) * (1.0 / 64.0) - base
    spots[0] = jnp.where(z >= slabs * CZ - 1, z - slabs * CZ, z)
    spots[1] = (code % (64 * ny)).astype(F32) * (1.0 / 64.0)


def hat(distance):
    return jnp.maximum(1 - jnp.abs(distance), 0)


def build(m, h, packed, spots, left, right):
    attrs = right.shape[0] // NX
    tiles = lax.axis_size("tile")
    ny = tiles * YT
    half = packed.shape[2] // LANES
    xs = [(iota(16, 0) + 16 * i).astype(F32).astype(BF16) for i in range(NX // 16)]
    ys = [(iota(YT, 0) + YT * t).astype(F32) for t in range(tiles)]
    zs = iota(2 * CZ, 0).astype(F32)
    first16, first8 = iota(16, 0) == 0, iota(YT, 0) == 0

    def block(q):
        at = pl.ds(pl.multiple_of(q * LANES, LANES), LANES)
        values = packed[m, :, at].astype(F32)[8 * h : 8 * h + 8]
        wide = [jnp.broadcast_to(values[c : c + 1], (16, LANES)) for c in range(8)]
        wrapped = jnp.where(first16 & (wide[6] > NX // 2), 1.0 * NX, iota(16, 0).astype(F32))
        col, frac = wide[6].astype(BF16), wide[7].astype(BF16)
        wx = [
            hat((wrapped.astype(BF16) if i == 0 else xs[i]) - col - frac) for i in range(NX // 16)
        ]
        for c in range(attrs):
            scale = wide[c].astype(BF16)
            for i in range(NX // 16):
                right[c * NX + 16 * i : c * NX + 16 * (i + 1), at] = wx[i] * scale
        z, y = (
            jnp.broadcast_to(spots[k, pl.ds(h * half + q, 1), :], (YT, LANES)) for k in range(2)
        )
        wz = hat(zs - z)
        wy = []
        for t in range(tiles):
            rows = ys[t]
            if t == 0:
                rows = jnp.where(first8 & (y > ny // 2), 1.0 * ny, rows)
            w = hat(rows - y)
            wy.append(jnp.concatenate([w, w], 0).astype(BF16))
        for k in range(0, 2 * CZ, 2):
            pair = jnp.concatenate(
                [jnp.broadcast_to(wz[k + i : k + i + 1], (YT, LANES)) for i in range(2)], 0
            ).astype(BF16)
            s, plane = k // CZ, k % CZ
            for t in range(tiles):
                row = (s * tiles + t) * CZ * YT + plane * YT
                left[row : row + 16, at] = pair * wy[t]

    if packed.shape[0] <= UNROLLED:
        for q in range(half):
            block(q)
    else:
        lax.fori_loop(0, half, lambda q, carry: block(q) or carry, 0)


def deposit(s, feat, dest, cell, code, live, arrive):
    slabs, tiles = lax.axis_size("slab"), lax.axis_size("tile")
    tile = lax.axis_index("tile")
    mine = lax.axis_index("slab") % 2
    group = slabs // 2
    attrs = feat.shape[0]
    pairs = attrs // 2
    size = CZ * YT
    tall = tiles * size
    lefts, rights = [s.left_a, s.left_b], [s.right_a, s.right_b]
    pack_particles(feat, dest, cell, code, live, s.packed, s.places)
    arrive()
    coming = [None]
    for m in range(1, group):
        device = flipped(2 * m)
        coming.append(
            [
                send(s.packed.at[0], s.packed.at[m], (s.send_p, s.recv_p), m, device),
                send(s.places.at[0], s.places.at[m], (s.send_q, s.recv_q), m, device),
            ]
        )

    def prepare(i):
        m, h = i // 2, i % 2
        if h == 0:
            if m:
                for copy in coming[m]:
                    copy.wait_recv()
            place_particles(m, s.places, s.spots.at[m % 2])
        build(m, h, s.packed, s.spots.at[m % 2], lefts[h], rights[h])

    def multiply(i, n):
        at = slice(2 * n * NX, (2 * n + 2) * NX)
        part = lax.dot_general(
            lefts[i % 2][...], rights[i % 2][at, :], NT, preferred_element_type=F32
        )
        if i == 0:
            s.total[:, at] = part
        else:
            s.total[:, at] += part

    def rows(which):
        return pl.ds(pl.multiple_of(which * tall, tall), tall)

    crossing, dealt = [], []

    def hand(n):
        for c in range(2):
            at = slice((2 * n + c) * NX, (2 * n + c + 1) * NX)
            s.outbox[n, c] = s.total[rows(1 - mine), at].astype(BF16)
        crossing.append(send(s.outbox.at[n], s.inbox.at[n], (s.send_c, s.recv_c), n, flipped(1)))

    def deal(n):
        crossing[n].wait_recv()
        for c in range(2):
            at = slice((2 * n + c) * NX, (2 * n + c + 1) * NX)
            total = s.total[rows(mine), at] + s.inbox[n, c].astype(F32)
            for t in range(tiles):
                s.sums[n, t, c] = total[t * size : (t + 1) * size].astype(BF16)
        dealt.append(
            [
                send(
                    s.sums.at[n, lax.rem(tile + d, tiles)],
                    s.last.at[n, d - 1],
                    (s.send_t, s.recv_t),
                    n * (tiles - 1) + d - 1,
                    ahead(d),
                )
                for d in range(1, tiles)
            ]
        )

    prepare(0)
    for i in range(2 * group):
        if i != 1 and i + 1 < 2 * group:
            prepare(i + 1)
        for n in range(pairs):
            multiply(i, n)
            if i == 2 * group - 1:
                hand(n)
                if n:
                    deal(n - 1)
        if i == 1:
            prepare(i + 1)
    deal(pairs - 1)
    s.block[...] = jnp.zeros_like(s.block)
    for n in range(pairs):
        for d in range(tiles - 1):
            dealt[n][d].wait_recv()
        for c in range(2):
            total = s.sums[n, tile, c].astype(F32)
            for d in range(tiles - 1):
                total = total + s.last[n, d, c].astype(F32)
            for z in range(CZ):
                s.block[z, :, 2 * n + c, :] = total[z * YT : (z + 1) * YT]
    for z in range(CZ):
        for y in range(YT // 2):
            s.grid[2 + z, 1 + y] = jnp.concatenate(
                [s.block[z, 2 * y], s.block[z, 2 * y + 1]], 0
            ).astype(BF16)
    return [copy for copies in coming[1:] for copy in copies] + crossing + sum(dealt, [])


def span(shift, size, width):
    if shift > 0:
        return pl.ds(size, width), pl.ds(0, width)
    if shift < 0:
        return pl.ds(width, width), pl.ds(size + width, width)
    return pl.ds(width, size), pl.ds(width, size)


def share_grid(s):
    copies = {}
    for n, (dz, dy) in enumerate(SIDES):
        from_z, to_z = span(dz, CZ, 2)
        from_y, to_y = span(dy, YT // 2, 1)
        copies[dz, dy] = send(
            s.grid.at[from_z, from_y],
            s.grid.at[to_z, to_y],
            (s.send_g, s.recv_g),
            n,
            neighbour(dz, dy),
        )
    return copies


def spread(values):
    return jnp.concatenate(
        [pltpu.roll(values, 1, 1), values, pltpu.roll(values, NX - 1, 1)], 0
    ).astype(BF16)


def cross(left, right):
    return lax.dot_general(left, right, (((0,), (0,)), ((), ())), preferred_element_type=F32)


def place(rows, columns, target_of):
    source = lax.broadcasted_iota(jnp.int32, (rows, columns), 0)
    target = lax.broadcasted_iota(jnp.int32, (rows, columns), 1)
    return jnp.where(target == target_of(source), 1.0, 0.0).astype(BF16)


def prepare_weights(s, lift_raw):
    taps = lift_raw.shape[2]
    each = taps // 3
    total = None
    for n in range(9):
        spots = place(taps, 216, lambda i: n * 24 + i // each * 8 + i % each)
        term = cross(lift_raw[n // 3, n % 3], spots)
        total = term if total is None else total + term
    s.lift[...] = total.astype(BF16)
    depth, tall = s.down_raw.shape[3:]
    for k in range(2):
        total = None
        for n in range(4):
            spots = place(depth, 4 * depth, lambda i: n * depth + i)
            term = cross(s.down_raw[n // 2, n % 2, k], spots)
            total = term if total is None else total + term
        s.down[k * tall : (k + 1) * tall] = total.astype(BF16)


def lift_level(s):
    planes, pairs = s.grid.shape[:2]
    for z in range(planes):
        for y in range(pairs):
            block = s.grid[z, y].astype(F32)
            before, after = pltpu.roll(block, 1, 1), pltpu.roll(block, NX - 1, 1)
            for p in range(2):
                at = slice(8 * p, 8 * p + 8)
                s.wide[z, 2 * y + p, 0:8] = before[at]
                s.wide[z, 2 * y + p, 8:16] = block[at]
                s.wide[z, 2 * y + p, 16:24] = after[at]
    rows = 2 * pairs - 2

    def lift_plane(z, carry):
        for y in range(0, rows, 2):
            pair = jnp.concatenate(
                [
                    jnp.concatenate(
                        [s.wide[z + a, y + p + b] for a in range(3) for b in range(3)], 0
                    ).astype(BF16)
                    for p in range(2)
                ],
                1,
            )
            values = act(dot(s.lift[...], pair))
            s.stack[z, y] = spread(values[:, :NX])
            s.stack[z, y + 1] = spread(values[:, NX:])
        return carry

    lax.fori_loop(0, planes - 2, lift_plane, 0)


def taps_of(weight):
    return [jnp.concatenate([weight[a, b] for a in range(3)], 0) for b in range(3)]


def conv_part(stack, lefts, acc, begun, z, j, bs):
    planes = stack.shape[0] - 2
    outs = lefts[0].shape[0] // 3
    part = None
    for b in bs:
        y = 2 * j + b
        term = dot(lefts[b], jnp.concatenate([stack[z, y], stack[z, y + 1]], 1))
        part = term if part is None else part + term
    for a in range(3):
        if 0 <= z - a < planes:
            piece = part[a * outs : (a + 1) * outs]
            if (z - a, j) in begun:
                acc[z - a, j] += piece
            else:
                acc[z - a, j] = piece
                begun.add((z - a, j))


def fine_level(s):
    lefts = taps_of(s.fine)
    source = iota(NX, 0)
    target = iota(NX, 1)
    half = NX // 2
    parity = jnp.where(target < half, 0, 1)
    sel = jnp.where(source == 2 * (target - half * parity) + parity, 1.0, 0.0).astype(BF16)
    chans = s.down.shape[0] // 2
    h = chans // 2
    lane = iota(h, 1)
    begun = set()
    copies = {}
    rows = YT // 2

    def share(key, from_z, from_y, to_z, to_y, side):
        copies[key] = send(
            s.low.at[from_z, from_y],
            s.low.at[to_z, to_y],
            (s.send_l, s.recv_l),
            len(copies),
            neighbour(*side),
        )

    for js in ((0, rows - 1), (1, rows - 2)):
        for j in js:
            for z in range(CZ + 2):
                conv_part(s.stack, lefts, s.acc, begun, z, j, range(3))
            for z in range(CZ):
                values = act(s.acc[z, j]).astype(BF16)
                s.second[z, 2 * j] = values[:, :NX]
                s.second[z, 2 * j + 1] = values[:, NX:]
        for z in range(CZ // 2):
            pair = []
            for j in js:
                tall = jnp.concatenate(
                    [s.second[2 * z + a, 2 * j + b] for a in range(2) for b in range(2)], 0
                )
                pair.append(dot(tall, sel).astype(BF16))
            out = dot(s.down[...], jnp.concatenate(pair, 1))
            for p in range(2):
                q = out[:, p * NX : (p + 1) * NX]
                q00, q01, q10, q11 = (q[i * h : (i + 1) * h] for i in range(4))
                row = jnp.where(lane < half, q00, q11) + pltpu.roll(
                    jnp.where(lane < half, q01, q10), half, 1
                )
                s.low[1 + z, 1 + js[p]] = act(row).astype(BF16)
        if js[0] == 0:
            for j, dy, to in ((0, -1, rows + 1), (rows - 1, 1, 0)):
                share((0, dy), pl.ds(1, 2), 1 + j, pl.ds(1, 2), to, (0, dy))
            for j, dy, to in ((0, -1, rows + 1), (rows - 1, 1, 0)):
                for dz in (-1, 1):
                    z, to_z = (1, 3) if dz < 0 else (2, 0)
                    share((dz, dy), z, 1 + j, to_z, to, (dz, dy))
            for j in js:
                for dz in (-1, 1):
                    z, to_z = (1, 3) if dz < 0 else (2, 0)
                    share((dz, 0, j), z, 1 + j, to_z, 1 + j, (dz, 0))
        else:
            for dz in (-1, 1):
                z, to_z = (1, 3) if dz < 0 else (2, 0)
                at = pl.ds(2, rows - 2)
                share((dz, 0, 1), z, at, to_z, at, (dz, 0))
    return copies


def coarse_level(s, copies):
    half = NX // 2
    chans = s.coarse.shape[2]
    outs = s.up.shape[3]
    lane = iota(chans // 2, 1)
    planes, rows = s.low.shape[:2]

    def columns(z, bs):
        row, turned, pairs = {}, {}, {}
        for r in sorted({2 * i + b + p for b in bs for i in range(2) for p in range(2)}):
            row[r] = s.low[z, r].astype(F32)
            turned[r] = pltpu.roll(row[r], half, 1)
        for r in sorted({2 * i + b for b in bs for i in range(2)}):
            top = jnp.where(lane < half, row[r], turned[r + 1])
            bottom = jnp.where(lane < half, turned[r], row[r + 1])
            pairs[r] = jnp.concatenate([top, bottom], 0).astype(BF16)
        for b in bs:
            s.columns[z, b] = jnp.concatenate([pairs[b], pairs[2 + b]], 1)

    def product(z, k, taps):
        return dot(
            jnp.concatenate([s.coarse[a, b, :, k * chans : (k + 1) * chans] for a, b in taps], 1),
            jnp.concatenate([s.columns[z + a, b] for a, b in taps], 0),
        )

    for z in (1, 2):
        columns(z, (1,))
    for z, at in ((0, (1, 2)), (1, (0, 1))):
        for k in range(3):
            s.part[z, k] = product(z, k, [(a, 1) for a in at])
    for key, copy in copies.items():
        if key[1] == 0:
            copy.wait_recv()
    for z in (0, 3):
        columns(z, (1,))
    for z, a in ((0, 0), (1, 2)):
        for k in range(3):
            s.part[z, k] += product(z, k, [(a, 1)])
    for key, copy in copies.items():
        if key[1]:
            copy.wait_recv()
    for z in range(planes):
        columns(z, (0, 2))

    source = lax.broadcasted_iota(jnp.int32, (NX, 4 * NX), 0)
    target = lax.broadcasted_iota(jnp.int32, (NX, 4 * NX), 1)
    spot = target % NX
    want = target // (2 * NX) * half + spot // 2
    sel = jnp.where((source == want) & (spot % 2 == target // NX % 2), 1.0, 0.0).astype(BF16)
    lane = iota(chans, 1)
    lefts = [
        jnp.concatenate([s.up[a, b, k] for a in range(2) for b in range(2)], 0) for k in range(2)
    ]
    onward = {}

    def share(key, from_z, from_y, to_z, to_y, side):
        onward[key] = send(
            s.joined.at[from_z, from_y],
            s.joined.at[to_z, to_y],
            (s.send_j, s.recv_j),
            len(onward),
            neighbour(*side),
        )

    for z in range(planes - 2):
        sides = [
            s.part[z, k] + product(z, k, [(a, b) for a in range(3) for b in (0, 2)])
            for k in range(3)
        ]
        for j in range(2):
            at = slice(j * NX, (j + 1) * NX)
            before, same, after = (side[:, at] for side in sides)
            before = jnp.where(
                lane % half == 0, pltpu.roll(before, half + 1, 1), pltpu.roll(before, 1, 1)
            )
            after = jnp.where(
                lane % half == half - 1,
                pltpu.roll(after, half - 1, 1),
                pltpu.roll(after, NX - 1, 1),
            )
            coarse = act(before + same + after).astype(BF16)
            wide = dot(coarse, sel).astype(BF16)
            right = [
                jnp.concatenate(
                    [wide[:, k * NX : (k + 1) * NX], wide[:, (2 + k) * NX : (3 + k) * NX]], 1
                )
                for k in range(2)
            ]
            raised = dot(lefts[0], right[0]) + dot(lefts[1], right[1])
            for a in range(2):
                for b in range(2):
                    for p in range(2):
                        y = 2 * (2 * j + p) + b
                        piece = raised[
                            (2 * a + b) * outs : (2 * a + b + 1) * outs, p * NX : (p + 1) * NX
                        ]
                        s.joined[1 + 2 * z + a, 1 + y] = (
                            s.second[2 * z + a, y].astype(F32) + piece
                        ).astype(BF16)
            dy, edge, to = ((-1, 1, YT + 1), (1, YT, 0))[j]
            dz, face, to_z = ((-1, 1, CZ + 1), (1, CZ, 0))[z]
            both = pl.ds(1 + 2 * z, 2)
            share((0, dy, z), both, edge, both, to, (0, dy))
            share((dz, dy), face, edge, to_z, to, (dz, dy))
            across = pl.ds(1 + 4 * j, 4)
            share((dz, 0, j), face, across, to_z, across, (dz, 0))
    return onward


def merge_level(s, copies, head, out):
    lefts = taps_of(s.merge)
    begun = set()
    last = YT // 2 - 1

    def widen(z, y):
        s.stack[z, y] = spread(s.joined[z, y].astype(F32))

    def inner(j):
        return [b for b in range(3) if (j, b) != (0, 0) and (j, b) != (last, 2)]

    for z in range(1, CZ + 1):
        for y in range(1, YT + 1):
            widen(z, y)
    for z in range(1, CZ + 1):
        for j in range(last + 1):
            conv_part(s.stack, lefts, s.acc, begun, z, j, inner(j))
    for key, copy in copies.items():
        if key[1] == 0:
            copy.wait_recv()
    for z in (0, CZ + 1):
        for y in range(1, YT + 1):
            widen(z, y)
        for j in range(last + 1):
            conv_part(s.stack, lefts, s.acc, begun, z, j, inner(j))
    for key, copy in copies.items():
        if key[1]:
            copy.wait_recv()
    for z in range(CZ + 2):
        for y in (0, YT + 1):
            widen(z, y)
        for j, b in ((0, 0), (last, 2)):
            conv_part(s.stack, lefts, s.acc, begun, z, j, [b])
    for z in range(CZ):
        for j in range(last + 1):
            moved = dot(head[...], act(s.acc[z, j]).astype(BF16))
            for p in range(2):
                out[:, z, 2 * j + p, :] = moved[: out.shape[0], p * NX : (p + 1) * NX]


FAR = ("fine", "down_raw", "coarse", "up", "merge")


def step_kernel(names, feat, dest, cell, code, live, lift_raw, head, *rest):
    far, out, scratch = rest[: len(FAR)], rest[len(FAR)], rest[len(FAR) + 1 :]
    s = types.SimpleNamespace(**dict(zip(names, scratch, strict=True)))
    slabs, tiles = lax.axis_size("slab"), lax.axis_size("tile")
    devices = [flipped(1)] + [flipped(2 * m) for m in range(1, slabs // 2)]
    devices += [ahead(d) for d in range(1, tiles)] + [neighbour(dz, dy) for dz, dy in SIDES]
    barrier = pltpu.get_barrier_semaphore()
    for device in devices:
        pl.semaphore_signal(barrier, inc=1, device_id=device, device_id_type=MESH)
    fetches = {}
    for n, name in enumerate(FAR):
        fetches[name] = pltpu.make_async_copy(far[n], getattr(s, name), s.fetched.at[n])
        fetches[name].start()

    def arrive():
        pl.semaphore_wait(barrier, len(devices))

    sent = deposit(s, feat, dest, cell, code, live, arrive)
    grids = share_grid(s)
    fetches["down_raw"].wait()
    prepare_weights(s, lift_raw)
    for copy in grids.values():
        copy.wait_recv()
    lift_level(s)
    fetches["fine"].wait()
    lows = fine_level(s)
    fetches["coarse"].wait()
    fetches["up"].wait()
    joins = coarse_level(s, lows)
    fetches["merge"].wait()
    merge_level(s, joins, head, out)
    for copy in sent + list(grids.values()) + list(lows.values()) + list(joins.values()):
        copy.wait_send()


def step(features, destination, cells, codes, live, lift, fine, down, coarse, up, merge, head):
    attrs, total = features.shape
    slabs, tiles = lax.axis_size("slab"), lax.axis_size("tile")
    size = CZ * YT
    group = slabs // 2
    pairs = attrs // 2
    outs, chans = fine.shape[2], coarse.shape[2]
    planes, rows = CZ + 2, YT + 2
    down = down.swapaxes(3, 4)

    def sems(count):
        return pltpu.SemaphoreType.DMA((count,))

    scratch = dict(
        packed=pltpu.VMEM((group, 16, total // 2), BF16),
        places=pltpu.VMEM((group, total // LANES, LANES), jnp.int32),
        spots=pltpu.VMEM((2, 2, total // LANES, LANES), F32),
        left_a=pltpu.VMEM((2 * tiles * size, total // 2), BF16),
        left_b=pltpu.VMEM((2 * tiles * size, total // 2), BF16),
        right_a=pltpu.VMEM((attrs * NX, total // 2), BF16),
        right_b=pltpu.VMEM((attrs * NX, total // 2), BF16),
        total=pltpu.VMEM((2 * tiles * size, attrs * NX), F32),
        outbox=pltpu.VMEM((pairs, 2, tiles * size, NX), BF16),
        inbox=pltpu.VMEM((pairs, 2, tiles * size, NX), BF16),
        sums=pltpu.VMEM((pairs, tiles, 2, size, NX), BF16),
        last=pltpu.VMEM((pairs, tiles - 1, 2, size, NX), BF16),
        block=pltpu.VMEM((CZ, YT, 8, NX), F32),
        grid=pltpu.VMEM((CZ + 4, YT // 2 + 2, 16, NX), BF16),
        wide=pltpu.VMEM((CZ + 4, YT + 4, 24, NX), F32),
        lift=pltpu.VMEM((outs, 216), BF16),
        down=pltpu.VMEM((2 * chans, 4 * outs), BF16),
        stack=pltpu.VMEM((planes, rows, 3 * outs, NX), BF16),
        acc=pltpu.VMEM((CZ, YT // 2, outs, 2 * NX), F32),
        second=pltpu.VMEM((CZ, YT, outs, NX), BF16),
        low=pltpu.VMEM((CZ // 2 + 2, YT // 2 + 2, chans // 2, NX), BF16),
        columns=pltpu.VMEM((CZ // 2 + 2, 3, chans, 2 * NX), BF16),
        part=pltpu.VMEM((CZ // 2, 3, chans, 2 * NX), F32),
        joined=pltpu.VMEM((planes, rows, outs, NX), BF16),
        fine=pltpu.VMEM(fine.shape, BF16),
        down_raw=pltpu.VMEM(down.shape, BF16),
        coarse=pltpu.VMEM(coarse.shape, BF16),
        up=pltpu.VMEM(up.shape, BF16),
        merge=pltpu.VMEM(merge.shape, BF16),
        fetched=sems(len(FAR)),
    )
    for name, count in dict(
        p=group, q=group, c=pairs, t=pairs * (tiles - 1), g=8, l=12, j=12
    ).items():
        scratch["send_" + name] = sems(count)
        scratch["recv_" + name] = sems(count)
    near = pl.BlockSpec(memory_space=pltpu.VMEM)
    far = pl.BlockSpec(memory_space=pl.ANY)

    def kernel(*refs):
        step_kernel(list(scratch), *refs)

    return pl.pallas_call(
        kernel,
        in_specs=[near] * 4 + [pl.BlockSpec(memory_space=pltpu.SMEM)] + [near] * 2 + [far] * 5,
        out_specs=near,
        out_shape=jax.ShapeDtypeStruct((head.shape[0], CZ, YT, NX), F32),
        scratch_shapes=list(scratch.values()),
        compiler_params=pltpu.CompilerParams(
            collective_id=0, has_side_effects=True, vmem_limit_bytes=60 << 20
        ),
        name="step",
    )(
        features,
        destination.reshape(-1, LANES),
        cells.reshape(-1, LANES),
        codes.reshape(-1, LANES),
        live,
        lift.swapaxes(2, 3),
        head,
        fine,
        down,
        coarse,
        up,
        merge,
    )


def solution(mesh):
    split = P(("slab", "tile"))
    placed = (P(None, ("slab", "tile")), P(("slab", "tile"), None)) + (split,) * 3 + (P(),) * 7
    return jax.shard_map(
        step, mesh=mesh, in_specs=placed, out_specs=P(None, "slab", "tile", None), check_vma=False
    )
```

```python
import types

import jax
import jax.numpy as jnp
from jax import lax
from jax.experimental import pallas as pl
from jax.experimental.pallas import tpu as pltpu
from jax.sharding import PartitionSpec as P

NX = 128
YT = 8
CZ = 4
LANES = 128
UNROLLED = 4


slope = 0.1


BF16 = jnp.bfloat16
F32 = jnp.float32
MESH = pl.DeviceIdType.MESH
NT = (((1,), (1,)), ((), ()))
SIDES = [(dz, dy) for dz in (-1, 0, 1) for dy in (-1, 0, 1) if dz or dy]


def act(values):
    return jnp.maximum(values, slope * values)


def dot(left, right):
    return jnp.dot(left, right, preferred_element_type=F32)


def neighbour(dz, dy):
    slabs, tiles = lax.axis_size("slab"), lax.axis_size("tile")
    return (
        lax.rem(lax.axis_index("slab") + (dz + slabs), slabs),
        lax.rem(lax.axis_index("tile") + (dy + tiles), tiles),
    )


def flipped(mask):
    slab = lax.axis_index("slab")
    other = slab
    for b in range(mask.bit_length()):
        if mask >> b & 1:
            other = other + 2**b * (1 - 2 * (slab // 2**b % 2))
    return other, lax.axis_index("tile")


def ahead(d):
    return lax.axis_index("slab"), lax.rem(lax.axis_index("tile") + d, lax.axis_size("tile"))


def send(source, target, sems, at, device):
    copy = pltpu.make_async_remote_copy(
        src_ref=source,
        dst_ref=target,
        send_sem=sems[0].at[at],
        recv_sem=sems[1].at[at],
        device_id=device,
        device_id_type=MESH,
    )
    copy.start()
    return copy


def iota(rows, axis):
    return lax.broadcasted_iota(jnp.int32, (rows, LANES), axis)


def pack_particles(feat, dest, cell, code, live, packed, places):
    attrs = feat.shape[0]
    ny = lax.axis_size("tile") * YT
    cells, codes = cell[...], code[...]
    row = cells // NX
    high = (dest[...] * CZ + row // ny) * 64 + ((codes >> 12) & 63)
    places[0] = high * (64 * ny) + (row % ny) * 64 + ((codes >> 6) & 63)
    col = (cells % NX).astype(F32)
    frac = (codes & 63).astype(F32) * (1.0 / 64.0)
    count = cells.shape[0]
    half = count // 2
    lane = lax.broadcasted_iota(jnp.int32, (attrs, LANES), 1)
    for q in range(half):
        rows = []
        for r in (q, half + q):
            values = feat[:, r * LANES : (r + 1) * LANES].astype(F32)
            rows.append(jnp.where(lane + r * LANES < live[...], values, 0.0))
            rows.append(col[r : r + 1])
            rows.append(frac[r : r + 1])
        packed[0, :, q * LANES : (q + 1) * LANES] = jnp.concatenate(rows, 0).astype(BF16)


def place_particles(m, places, spots):
    slabs, ny = lax.axis_size("slab"), lax.axis_size("tile") * YT
    base = (lax.axis_index("slab") // 2 * (2 * CZ)).astype(F32)
    code = places[m]
    z = (code // (64 * ny)).astype(F32) * (1.0 / 64.0) - base
    spots[0] = jnp.where(z >= slabs * CZ - 1, z - slabs * CZ, z)
    spots[1] = (code % (64 * ny)).astype(F32) * (1.0 / 64.0)


def hat(distance):
    return jnp.maximum(1 - jnp.abs(distance), 0)


def build(m, h, packed, spots, left, right):
    attrs = right.shape[0] // NX
    tiles = lax.axis_size("tile")
    ny = tiles * YT
    half = packed.shape[2] // LANES
    xs = [(iota(16, 0) + 16 * i).astype(F32).astype(BF16) for i in range(NX // 16)]
    ys = [(iota(YT, 0) + YT * t).astype(F32) for t in range(tiles)]
    zs = iota(2 * CZ, 0).astype(F32)
    first16, first8 = iota(16, 0) == 0, iota(YT, 0) == 0

    def block(q):
        at = pl.ds(pl.multiple_of(q * LANES, LANES), LANES)
        values = packed[m, :, at].astype(F32)[8 * h : 8 * h + 8]
        wide = [jnp.broadcast_to(values[c : c + 1], (16, LANES)) for c in range(8)]
        wrapped = jnp.where(first16 & (wide[6] > NX // 2), 1.0 * NX, iota(16, 0).astype(F32))
        col, frac = wide[6].astype(BF16), wide[7].astype(BF16)
        wx = [
            hat((wrapped.astype(BF16) if i == 0 else xs[i]) - col - frac) for i in range(NX // 16)
        ]
        for c in range(attrs):
            scale = wide[c].astype(BF16)
            for i in range(NX // 16):
                right[c * NX + 16 * i : c * NX + 16 * (i + 1), at] = wx[i] * scale
        z, y = (
            jnp.broadcast_to(spots[k, pl.ds(h * half + q, 1), :], (YT, LANES)) for k in range(2)
        )
        wz = hat(zs - z)
        wy = []
        for t in range(tiles):
            rows = ys[t]
            if t == 0:
                rows = jnp.where(first8 & (y > ny // 2), 1.0 * ny, rows)
            w = hat(rows - y)
            wy.append(jnp.concatenate([w, w], 0).astype(BF16))
        for k in range(0, 2 * CZ, 2):
            pair = jnp.concatenate(
                [jnp.broadcast_to(wz[k + i : k + i + 1], (YT, LANES)) for i in range(2)], 0
            ).astype(BF16)
            s, plane = k // CZ, k % CZ
            for t in range(tiles):
                row = (s * tiles + t) * CZ * YT + plane * YT
                left[row : row + 16, at] = pair * wy[t]

    if packed.shape[0] <= UNROLLED:
        for q in range(half):
            block(q)
    else:
        lax.fori_loop(0, half, lambda q, carry: block(q) or carry, 0)


def deposit(s, feat, dest, cell, code, live, arrive):
    slabs, tiles = lax.axis_size("slab"), lax.axis_size("tile")
    tile = lax.axis_index("tile")
    mine = lax.axis_index("slab") % 2
    group = slabs // 2
    attrs = feat.shape[0]
    pairs = attrs // 2
    size = CZ * YT
    tall = tiles * size
    lefts, rights = [s.left_a, s.left_b], [s.right_a, s.right_b]
    pack_particles(feat, dest, cell, code, live, s.packed, s.places)
    arrive()
    coming = [None]
    for m in range(1, group):
        device = flipped(2 * m)
        coming.append(
            [
                send(s.packed.at[0], s.packed.at[m], (s.send_p, s.recv_p), m, device),
                send(s.places.at[0], s.places.at[m], (s.send_q, s.recv_q), m, device),
            ]
        )

    def prepare(i):
        m, h = i // 2, i % 2
        if h == 0:
            if m:
                for copy in coming[m]:
                    copy.wait_recv()
            place_particles(m, s.places, s.spots.at[m % 2])
        build(m, h, s.packed, s.spots.at[m % 2], lefts[h], rights[h])

    def multiply(i, n):
        at = slice(2 * n * NX, (2 * n + 2) * NX)
        part = lax.dot_general(
            lefts[i % 2][...], rights[i % 2][at, :], NT, preferred_element_type=F32
        )
        if i == 0:
            s.total[:, at] = part
        else:
            s.total[:, at] += part

    def rows(which):
        return pl.ds(pl.multiple_of(which * tall, tall), tall)

    crossing, dealt = [], []

    def hand(n):
        for c in range(2):
            at = slice((2 * n + c) * NX, (2 * n + c + 1) * NX)
            s.outbox[n, c] = s.total[rows(1 - mine), at].astype(BF16)
        crossing.append(send(s.outbox.at[n], s.inbox.at[n], (s.send_c, s.recv_c), n, flipped(1)))

    def deal(n):
        crossing[n].wait_recv()
        for c in range(2):
            at = slice((2 * n + c) * NX, (2 * n + c + 1) * NX)
            total = s.total[rows(mine), at] + s.inbox[n, c].astype(F32)
            for t in range(tiles):
                s.sums[n, t, c] = total[t * size : (t + 1) * size].astype(BF16)
        dealt.append(
            [
                send(
                    s.sums.at[n, lax.rem(tile + d, tiles)],
                    s.last.at[n, d - 1],
                    (s.send_t, s.recv_t),
                    n * (tiles - 1) + d - 1,
                    ahead(d),
                )
                for d in range(1, tiles)
            ]
        )

    prepare(0)
    for i in range(2 * group):
        if i != 1 and i + 1 < 2 * group:
            prepare(i + 1)
        for n in range(pairs):
            multiply(i, n)
            if i == 2 * group - 1:
                hand(n)
                if n:
                    deal(n - 1)
        if i == 1:
            prepare(i + 1)
    deal(pairs - 1)
    s.block[...] = jnp.zeros_like(s.block)
    for n in range(pairs):
        for d in range(tiles - 1):
            dealt[n][d].wait_recv()
        for c in range(2):
            total = s.sums[n, tile, c].astype(F32)
            for d in range(tiles - 1):
                total = total + s.last[n, d, c].astype(F32)
            for z in range(CZ):
                s.block[z, :, 2 * n + c, :] = total[z * YT : (z + 1) * YT]
    for z in range(CZ):
        for y in range(YT // 2):
            s.grid[2 + z, 1 + y] = jnp.concatenate(
                [s.block[z, 2 * y], s.block[z, 2 * y + 1]], 0
            ).astype(BF16)
    return [copy for copies in coming[1:] for copy in copies] + crossing + sum(dealt, [])


def span(shift, size, width):
    if shift > 0:
        return pl.ds(size, width), pl.ds(0, width)
    if shift < 0:
        return pl.ds(width, width), pl.ds(size + width, width)
    return pl.ds(width, size), pl.ds(width, size)


def share_grid(s):
    copies = {}
    for n, (dz, dy) in enumerate(SIDES):
        from_z, to_z = span(dz, CZ, 2)
        from_y, to_y = span(dy, YT // 2, 1)
        copies[dz, dy] = send(
            s.grid.at[from_z, from_y],
            s.grid.at[to_z, to_y],
            (s.send_g, s.recv_g),
            n,
            neighbour(dz, dy),
        )
    return copies


def spread(values):
    return jnp.concatenate(
        [pltpu.roll(values, 1, 1), values, pltpu.roll(values, NX - 1, 1)], 0
    ).astype(BF16)


def cross(left, right):
    return lax.dot_general(left, right, (((0,), (0,)), ((), ())), preferred_element_type=F32)


def place(rows, columns, target_of):
    source = lax.broadcasted_iota(jnp.int32, (rows, columns), 0)
    target = lax.broadcasted_iota(jnp.int32, (rows, columns), 1)
    return jnp.where(target == target_of(source), 1.0, 0.0).astype(BF16)


def prepare_weights(s, lift_raw):
    taps = lift_raw.shape[2]
    each = taps // 3
    total = None
    for n in range(9):
        spots = place(taps, 216, lambda i: n * 24 + i // each * 8 + i % each)
        term = cross(lift_raw[n // 3, n % 3], spots)
        total = term if total is None else total + term
    s.lift[...] = total.astype(BF16)
    depth, tall = s.down_raw.shape[3:]
    for k in range(2):
        total = None
        for n in range(4):
            spots = place(depth, 4 * depth, lambda i: n * depth + i)
            term = cross(s.down_raw[n // 2, n % 2, k], spots)
            total = term if total is None else total + term
        s.down[k * tall : (k + 1) * tall] = total.astype(BF16)


def lift_level(s):
    planes, pairs = s.grid.shape[:2]
    for z in range(planes):
        for y in range(pairs):
            block = s.grid[z, y].astype(F32)
            before, after = pltpu.roll(block, 1, 1), pltpu.roll(block, NX - 1, 1)
            for p in range(2):
                at = slice(8 * p, 8 * p + 8)
                s.wide[z, 2 * y + p, 0:8] = before[at]
                s.wide[z, 2 * y + p, 8:16] = block[at]
                s.wide[z, 2 * y + p, 16:24] = after[at]
    rows = 2 * pairs - 2

    def lift_plane(z, carry):
        for y in range(0, rows, 2):
            pair = jnp.concatenate(
                [
                    jnp.concatenate(
                        [s.wide[z + a, y + p + b] for a in range(3) for b in range(3)], 0
                    ).astype(BF16)
                    for p in range(2)
                ],
                1,
            )
            values = act(dot(s.lift[...], pair))
            s.stack[z, y] = spread(values[:, :NX])
            s.stack[z, y + 1] = spread(values[:, NX:])
        return carry

    lax.fori_loop(0, planes - 2, lift_plane, 0, unroll=True)


def taps_of(weight):
    return [jnp.concatenate([weight[a, b] for a in range(3)], 0) for b in range(3)]


def conv_part(stack, lefts, acc, begun, z, j, bs):
    planes = stack.shape[0] - 2
    outs = lefts[0].shape[0] // 3
    part = None
    for b in bs:
        y = 2 * j + b
        term = dot(lefts[b], jnp.concatenate([stack[z, y], stack[z, y + 1]], 1))
        part = term if part is None else part + term
    for a in range(3):
        if 0 <= z - a < planes:
            piece = part[a * outs : (a + 1) * outs]
            if (z - a, j) in begun:
                acc[z - a, j] += piece
            else:
                acc[z - a, j] = piece
                begun.add((z - a, j))


def fine_level(s):
    lefts = taps_of(s.fine)
    source = iota(NX, 0)
    target = iota(NX, 1)
    half = NX // 2
    parity = jnp.where(target < half, 0, 1)
    sel = jnp.where(source == 2 * (target - half * parity) + parity, 1.0, 0.0).astype(BF16)
    chans = s.down.shape[0] // 2
    h = chans // 2
    lane = iota(h, 1)
    begun = set()
    copies = {}
    rows = YT // 2
    mine = lax.axis_index("slab") % 2

    def share(key, from_z, from_y, to_z, to_y, side):
        copies[key] = send(
            s.low.at[from_z, from_y],
            s.low.at[to_z, to_y],
            (s.send_l, s.recv_l),
            len(copies),
            neighbour(*side),
        )

    for js in ((0, rows - 1), (1, rows - 2)):
        for j in js:
            for z in range(CZ + 2):
                conv_part(s.stack, lefts, s.acc, begun, z, j, range(3))
            for z in range(CZ):
                values = act(s.acc[z, j]).astype(BF16)
                s.second[z, 2 * j] = values[:, :NX]
                s.second[z, 2 * j + 1] = values[:, NX:]
        for z in range(CZ // 2):
            pair = []
            for j in js:
                tall = jnp.concatenate(
                    [s.second[2 * z + a, 2 * j + b] for a in range(2) for b in range(2)], 0
                )
                pair.append(dot(tall, sel).astype(BF16))
            out = dot(s.down[...], jnp.concatenate(pair, 1))
            for p in range(2):
                q = out[:, p * NX : (p + 1) * NX]
                q00, q01, q10, q11 = (q[i * h : (i + 1) * h] for i in range(4))
                row = jnp.where(lane < half, q00, q11) + pltpu.roll(
                    jnp.where(lane < half, q01, q10), half, 1
                )
                s.low[1 + z, 1 + js[p]] = act(row).astype(BF16)
        if js[0] == 0:
            for j, dy, to in ((0, -1, rows + 1), (rows - 1, 1, 0)):
                share((0, dy), pl.ds(1, 2), 1 + j, pl.ds(1, 2), to, (0, dy))
            for j, dy, to in ((0, -1, rows + 1), (rows - 1, 1, 0)):
                share((2, dy), 1 + mine, 1 + j, 3 * (1 - mine), to, (2 * mine - 1, dy))
            for j in js:
                for dz in (-1, 1):
                    z, to_z = (1, 3) if dz < 0 else (2, 0)
                    share((dz, 0, j), z, 1 + j, to_z, 1 + j, (dz, 0))
        else:
            for dz in (-1, 1):
                z, to_z = (1, 3) if dz < 0 else (2, 0)
                at = pl.ds(2, rows - 2)
                share((dz, 0, 1), z, at, to_z, at, (dz, 0))
    return copies


def wait_some(copies, chosen):
    for key, copy in copies.items():
        if chosen(key):
            copy.wait_recv()


def pass_on(padded, s, first):
    planes, rows = padded.shape[:2]
    mine = lax.axis_index("slab") % 2
    z, to_z = planes - 2 - (planes - 3) * mine, (planes - 1) * mine
    return [
        send(padded.at[z, y], padded.at[to_z, y], (s.send_w, s.recv_w), first + i, flipped(1))
        for i, y in enumerate((0, rows - 1))
    ]


def coarse_level(s, copies):
    half = NX // 2
    chans = s.coarse.shape[2]
    outs = s.up.shape[3]
    lane = iota(chans // 2, 1)
    planes, rows = s.low.shape[:2]

    def columns(z):
        row = {r: s.low[z, r].astype(F32) for r in range(1, rows - 1)}
        turned = {r: pltpu.roll(row[r], half, 1) for r in row}
        blank = jnp.zeros_like(row[1])
        for r in (0, rows - 1):
            row[r] = turned[r] = blank
        pairs = []
        for r in range(rows - 1):
            top = jnp.where(lane < half, row[r], turned[r + 1])
            bottom = jnp.where(lane < half, turned[r], row[r + 1])
            pairs.append(jnp.concatenate([top, bottom], 0).astype(BF16))
        for b in range(3):
            s.columns[z, b] = jnp.concatenate([pairs[b], pairs[2 + b]], 1)

    def edges(z):
        low, high = (s.low[z, r].astype(F32) for r in (0, rows - 1))
        blank = jnp.zeros_like(low)
        first = [jnp.where(lane < half, v, blank) for v in (low, pltpu.roll(low, half, 1))]
        second = [jnp.where(lane < half, blank, v) for v in (pltpu.roll(high, half, 1), high)]
        return [jnp.concatenate(v, 0).astype(BF16) for v in (first, second)]

    def weights(k, taps):
        return jnp.concatenate(
            [s.coarse[a, b, :, k * chans : (k + 1) * chans] for a, b in taps], 1
        )

    def product(z, k, taps):
        return dot(
            weights(k, taps), jnp.concatenate([s.columns[z + a, b] for a, b in taps], 0)
        )

    for z in (1, 2):
        columns(z)
    for z, at in ((0, (1, 2)), (1, (0, 1))):
        for k in range(3):
            s.part[z, k] = product(z, k, [(a, b) for a in at for b in range(3)])
    for key, copy in copies.items():
        if key[1] == 0:
            copy.wait_recv()
    for z in (0, 3):
        columns(z)
    for z, a in ((0, 0), (1, 2)):
        for k in range(3):
            s.part[z, k] += product(z, k, [(a, b) for b in range(3)])
    wait_some(copies, lambda key: key[0] == 0)
    passed = pass_on(s.low, s, 0)
    wait_some(copies, lambda key: key[0] == 2)
    for copy in passed:
        copy.wait_recv()
    edge = [edges(z) for z in range(planes)]
    outer = jnp.concatenate(
        [
            jnp.concatenate([edge[a][i], edge[a + 1][i]], 1)
            for a in range(3)
            for i in range(2)
        ],
        0,
    )
    halos = [dot(weights(k, [(a, b) for a in range(3) for b in (0, 2)]), outer) for k in range(3)]

    source = lax.broadcasted_iota(jnp.int32, (NX, 4 * NX), 0)
    target = lax.broadcasted_iota(jnp.int32, (NX, 4 * NX), 1)
    spot = target % NX
    want = target // (2 * NX) * half + spot // 2
    sel = jnp.where((source == want) & (spot % 2 == target // NX % 2), 1.0, 0.0).astype(BF16)
    lane = iota(chans, 1)
    lefts = [
        jnp.concatenate([s.up[a, b, k] for a in range(2) for b in range(2)], 0) for k in range(2)
    ]
    onward = {}
    mine = lax.axis_index("slab") % 2

    def share(key, from_z, from_y, to_z, to_y, side):
        onward[key] = send(
            s.joined.at[from_z, from_y],
            s.joined.at[to_z, to_y],
            (s.send_j, s.recv_j),
            len(onward),
            neighbour(*side),
        )

    for z in range(planes - 2):
        for j in range(2):
            at = slice(j * NX, (j + 1) * NX)
            own = lane < half if j == 0 else lane >= half
            before, same, after = (
                s.part[z, k, :, at]
                + jnp.where(own, halos[k][:, z * NX : (z + 1) * NX], 0.0)
                for k in range(3)
            )
            before = jnp.where(
                lane % half == 0, pltpu.roll(before, half + 1, 1), pltpu.roll(before, 1, 1)
            )
            after = jnp.where(
                lane % half == half - 1,
                pltpu.roll(after, half - 1, 1),
                pltpu.roll(after, NX - 1, 1),
            )
            coarse = act(before + same + after).astype(BF16)
            wide = dot(coarse, sel).astype(BF16)
            right = [
                jnp.concatenate(
                    [wide[:, k * NX : (k + 1) * NX], wide[:, (2 + k) * NX : (3 + k) * NX]], 1
                )
                for k in range(2)
            ]
            raised = dot(lefts[0], right[0]) + dot(lefts[1], right[1])
            for a in range(2):
                for b in range(2):
                    for p in range(2):
                        y = 2 * (2 * j + p) + b
                        piece = raised[
                            (2 * a + b) * outs : (2 * a + b + 1) * outs, p * NX : (p + 1) * NX
                        ]
                        s.joined[1 + 2 * z + a, 1 + y] = (
                            s.second[2 * z + a, y].astype(F32) + piece
                        ).astype(BF16)
            dy, edge, to = ((-1, 1, YT + 1), (1, YT, 0))[j]
            dz, face, to_z = ((-1, 1, CZ + 1), (1, CZ, 0))[z]
            both = pl.ds(1 + 2 * z, 2)
            share((0, dy, z), both, edge, both, to, (0, dy))
            if z:
                away = 5 * (1 - mine)
                share((2, dy), 1 + 3 * mine, edge, away, to, (2 * mine - 1, dy))
            across = pl.ds(1 + 4 * j, 4)
            share((dz, 0, j), face, across, to_z, across, (dz, 0))
    return onward, passed


def merge_level(s, copies, head, out):
    lefts = taps_of(s.merge)
    begun = set()
    last = YT // 2 - 1

    def widen(z, y):
        s.stack[z, y] = spread(s.joined[z, y].astype(F32))

    def inner(j):
        return [b for b in range(3) if (j, b) != (0, 0) and (j, b) != (last, 2)]

    for z in range(1, CZ + 1):
        for y in range(1, YT + 1):
            widen(z, y)
    for z in range(1, CZ + 1):
        for j in range(last + 1):
            conv_part(s.stack, lefts, s.acc, begun, z, j, inner(j))
    for key, copy in copies.items():
        if key[1] == 0:
            copy.wait_recv()
    for z in (0, CZ + 1):
        for y in range(1, YT + 1):
            widen(z, y)
        for j in range(last + 1):
            conv_part(s.stack, lefts, s.acc, begun, z, j, inner(j))
    wait_some(copies, lambda key: key[0] == 0)
    passed = pass_on(s.joined, s, 2)

    def outer(planes):
        for z in planes:
            for y in (0, YT + 1):
                widen(z, y)
            for j, b in ((0, 0), (last, 2)):
                conv_part(s.stack, lefts, s.acc, begun, z, j, [b])

    outer(range(1, CZ + 1))
    wait_some(copies, lambda key: key[0] == 2)
    for copy in passed:
        copy.wait_recv()
    outer((0, CZ + 1))
    for z in range(CZ):
        for j in range(last + 1):
            moved = dot(head[...], act(s.acc[z, j]).astype(BF16))
            for p in range(2):
                out[:, z, 2 * j + p, :] = moved[: out.shape[0], p * NX : (p + 1) * NX]
    return passed


FAR = ("fine", "down_raw", "coarse", "up", "merge")


def step_kernel(names, feat, dest, cell, code, live, lift_raw, head, *rest):
    far, out, scratch = rest[: len(FAR)], rest[len(FAR)], rest[len(FAR) + 1 :]
    s = types.SimpleNamespace(**dict(zip(names, scratch, strict=True)))
    slabs, tiles = lax.axis_size("slab"), lax.axis_size("tile")
    devices = [flipped(1)] + [flipped(2 * m) for m in range(1, slabs // 2)]
    devices += [ahead(d) for d in range(1, tiles)] + [neighbour(dz, dy) for dz, dy in SIDES]
    barrier = pltpu.get_barrier_semaphore()
    for device in devices:
        pl.semaphore_signal(barrier, inc=1, device_id=device, device_id_type=MESH)
    fetches = {}
    for n, name in enumerate(FAR):
        fetches[name] = pltpu.make_async_copy(far[n], getattr(s, name), s.fetched.at[n])
        fetches[name].start()

    def arrive():
        pl.semaphore_wait(barrier, len(devices))

    sent = deposit(s, feat, dest, cell, code, live, arrive)
    grids = share_grid(s)
    fetches["down_raw"].wait()
    prepare_weights(s, lift_raw)
    for copy in grids.values():
        copy.wait_recv()
    lift_level(s)
    fetches["fine"].wait()
    lows = fine_level(s)
    fetches["coarse"].wait()
    fetches["up"].wait()
    joins, passed = coarse_level(s, lows)
    fetches["merge"].wait()
    passed = passed + merge_level(s, joins, head, out)
    for copy in sent + passed + list(grids.values()) + list(lows.values()) + list(joins.values()):
        copy.wait_send()


def step(features, destination, cells, codes, live, lift, fine, down, coarse, up, merge, head):
    attrs, total = features.shape
    slabs, tiles = lax.axis_size("slab"), lax.axis_size("tile")
    size = CZ * YT
    group = slabs // 2
    pairs = attrs // 2
    outs, chans = fine.shape[2], coarse.shape[2]
    planes, rows = CZ + 2, YT + 2
    down = down.swapaxes(3, 4)

    def sems(count):
        return pltpu.SemaphoreType.DMA((count,))

    scratch = dict(
        packed=pltpu.VMEM((group, 16, total // 2), BF16),
        places=pltpu.VMEM((group, total // LANES, LANES), jnp.int32),
        spots=pltpu.VMEM((2, 2, total // LANES, LANES), F32),
        left_a=pltpu.VMEM((2 * tiles * size, total // 2), BF16),
        left_b=pltpu.VMEM((2 * tiles * size, total // 2), BF16),
        right_a=pltpu.VMEM((attrs * NX, total // 2), BF16),
        right_b=pltpu.VMEM((attrs * NX, total // 2), BF16),
        total=pltpu.VMEM((2 * tiles * size, attrs * NX), F32),
        outbox=pltpu.VMEM((pairs, 2, tiles * size, NX), BF16),
        inbox=pltpu.VMEM((pairs, 2, tiles * size, NX), BF16),
        sums=pltpu.VMEM((pairs, tiles, 2, size, NX), BF16),
        last=pltpu.VMEM((pairs, tiles - 1, 2, size, NX), BF16),
        block=pltpu.VMEM((CZ, YT, 8, NX), F32),
        grid=pltpu.VMEM((CZ + 4, YT // 2 + 2, 16, NX), BF16),
        wide=pltpu.VMEM((CZ + 4, YT + 4, 24, NX), F32),
        lift=pltpu.VMEM((outs, 216), BF16),
        down=pltpu.VMEM((2 * chans, 4 * outs), BF16),
        stack=pltpu.VMEM((planes, rows, 3 * outs, NX), BF16),
        acc=pltpu.VMEM((CZ, YT // 2, outs, 2 * NX), F32),
        second=pltpu.VMEM((CZ, YT, outs, NX), BF16),
        low=pltpu.VMEM((CZ // 2 + 2, YT // 2 + 2, chans // 2, NX), BF16),
        columns=pltpu.VMEM((CZ // 2 + 2, 3, chans, 2 * NX), BF16),
        part=pltpu.VMEM((CZ // 2, 3, chans, 2 * NX), F32),
        joined=pltpu.VMEM((planes, rows, outs, NX), BF16),
        fine=pltpu.VMEM(fine.shape, BF16),
        down_raw=pltpu.VMEM(down.shape, BF16),
        coarse=pltpu.VMEM(coarse.shape, BF16),
        up=pltpu.VMEM(up.shape, BF16),
        merge=pltpu.VMEM(merge.shape, BF16),
        fetched=sems(len(FAR)),
    )
    for name, count in dict(
        p=group, q=group, c=pairs, t=pairs * (tiles - 1), g=8, l=10, j=10, w=4
    ).items():
        scratch["send_" + name] = sems(count)
        scratch["recv_" + name] = sems(count)
    near = pl.BlockSpec(memory_space=pltpu.VMEM)
    far = pl.BlockSpec(memory_space=pl.ANY)

    def kernel(*refs):
        step_kernel(list(scratch), *refs)

    return pl.pallas_call(
        kernel,
        in_specs=[near] * 7 + [far] * 5,
        out_specs=near,
        out_shape=jax.ShapeDtypeStruct((head.shape[0], CZ, YT, NX), F32),
        scratch_shapes=list(scratch.values()),
        compiler_params=pltpu.CompilerParams(
            collective_id=0, has_side_effects=True, vmem_limit_bytes=60 << 20
        ),
        name="step",
    )(
        features,
        destination.reshape(-1, LANES),
        cells.reshape(-1, LANES),
        codes.reshape(-1, LANES),
        live.reshape(1, 1),
        lift.swapaxes(2, 3),
        head,
        fine,
        down,
        coarse,
        up,
        merge,
    )


def solution(mesh):
    split = P(("slab", "tile"))
    placed = (P(None, ("slab", "tile")), P(("slab", "tile"), None)) + (split,) * 3 + (P(),) * 7
    return jax.shard_map(
        step, mesh=mesh, in_specs=placed, out_specs=P(None, "slab", "tile", None), check_vma=False
    )
```

```python
import types

import jax
import jax.numpy as jnp
from jax import lax
from jax.experimental import pallas as pl
from jax.experimental.pallas import tpu as pltpu
from jax.sharding import PartitionSpec as P

NX = 128
YT = 8
CZ = 4
LANES = 128
UNROLLED = 4


slope = 0.1


BF16 = jnp.bfloat16
F32 = jnp.float32
MESH = pl.DeviceIdType.MESH
NT = (((1,), (1,)), ((), ()))
SIDES = [(dz, dy) for dz in (-1, 0, 1) for dy in (-1, 0, 1) if dz or dy]


def act(values):
    return jnp.maximum(values, slope * values)


def dot(left, right):
    return jnp.dot(left, right, preferred_element_type=F32)


def neighbour(dz, dy):
    slabs, tiles = lax.axis_size("slab"), lax.axis_size("tile")
    return (
        lax.rem(lax.axis_index("slab") + (dz + slabs), slabs),
        lax.rem(lax.axis_index("tile") + (dy + tiles), tiles),
    )


def flipped(mask):
    slab = lax.axis_index("slab")
    other = slab
    for b in range(mask.bit_length()):
        if mask >> b & 1:
            other = other + 2**b * (1 - 2 * (slab // 2**b % 2))
    return other, lax.axis_index("tile")


def ahead(d):
    return lax.axis_index("slab"), lax.rem(lax.axis_index("tile") + d, lax.axis_size("tile"))


def send(source, target, sems, at, device):
    copy = pltpu.make_async_remote_copy(
        src_ref=source,
        dst_ref=target,
        send_sem=sems[0].at[at],
        recv_sem=sems[1].at[at],
        device_id=device,
        device_id_type=MESH,
    )
    copy.start()
    return copy


def iota(rows, axis):
    return lax.broadcasted_iota(jnp.int32, (rows, LANES), axis)


def pack_particles(feat, dest, cell, code, live, packed, places):
    attrs = feat.shape[0]
    ny = lax.axis_size("tile") * YT
    cells, codes = cell[...], code[...]
    row = cells // NX
    high = (dest[...] * CZ + row // ny) * 64 + ((codes >> 12) & 63)
    places[0] = high * (64 * ny) + (row % ny) * 64 + ((codes >> 6) & 63)
    col = (cells % NX).astype(F32)
    frac = (codes & 63).astype(F32) * (1.0 / 64.0)
    count = cells.shape[0]
    half = count // 2
    lane = lax.broadcasted_iota(jnp.int32, (attrs, LANES), 1)
    for q in range(half):
        rows = []
        for r in (q, half + q):
            values = feat[:, r * LANES : (r + 1) * LANES].astype(F32)
            rows.append(jnp.where(lane + r * LANES < live[...], values, 0.0))
            rows.append(col[r : r + 1])
            rows.append(frac[r : r + 1])
        packed[0, :, q * LANES : (q + 1) * LANES] = jnp.concatenate(rows, 0).astype(BF16)


def place_particles(m, places, spots):
    slabs, ny = lax.axis_size("slab"), lax.axis_size("tile") * YT
    base = (lax.axis_index("slab") // 2 * (2 * CZ)).astype(F32)
    code = places[m]
    z = (code // (64 * ny)).astype(F32) * (1.0 / 64.0) - base
    spots[0] = jnp.where(z >= slabs * CZ - 1, z - slabs * CZ, z)
    spots[1] = (code % (64 * ny)).astype(F32) * (1.0 / 64.0)


def hat(distance):
    return jnp.maximum(1 - jnp.abs(distance), 0)


def build(m, h, packed, spots, left, right):
    attrs = right.shape[0] // NX
    tiles = lax.axis_size("tile")
    ny = tiles * YT
    half = packed.shape[2] // LANES
    xs = [(iota(16, 0) + 16 * i).astype(F32).astype(BF16) for i in range(NX // 16)]
    ys = [(iota(YT, 0) + YT * t).astype(F32) for t in range(tiles)]
    zs = iota(2 * CZ, 0).astype(F32)
    first16, first8 = iota(16, 0) == 0, iota(YT, 0) == 0

    def block(q):
        at = pl.ds(pl.multiple_of(q * LANES, LANES), LANES)
        values = packed[m, :, at].astype(F32)[8 * h : 8 * h + 8]
        wide = [jnp.broadcast_to(values[c : c + 1], (16, LANES)) for c in range(8)]
        wrapped = jnp.where(first16 & (wide[6] > NX // 2), 1.0 * NX, iota(16, 0).astype(F32))
        col, frac = wide[6].astype(BF16), wide[7].astype(BF16)
        wx = [
            hat((wrapped.astype(BF16) if i == 0 else xs[i]) - col - frac) for i in range(NX // 16)
        ]
        for c in range(attrs):
            scale = wide[c].astype(BF16)
            for i in range(NX // 16):
                right[c * NX + 16 * i : c * NX + 16 * (i + 1), at] = wx[i] * scale
        z, y = (
            jnp.broadcast_to(spots[k, pl.ds(h * half + q, 1), :], (YT, LANES)) for k in range(2)
        )
        wz = hat(zs - z)
        wy = []
        for t in range(tiles):
            rows = ys[t]
            if t == 0:
                rows = jnp.where(first8 & (y > ny // 2), 1.0 * ny, rows)
            w = hat(rows - y)
            wy.append(jnp.concatenate([w, w], 0).astype(BF16))
        for k in range(0, 2 * CZ, 2):
            pair = jnp.concatenate(
                [jnp.broadcast_to(wz[k + i : k + i + 1], (YT, LANES)) for i in range(2)], 0
            ).astype(BF16)
            s, plane = k // CZ, k % CZ
            for t in range(tiles):
                row = (s * tiles + t) * CZ * YT + plane * YT
                left[row : row + 16, at] = pair * wy[t]

    if packed.shape[0] <= UNROLLED:
        for q in range(half):
            block(q)
    else:
        lax.fori_loop(0, half, lambda q, carry: block(q) or carry, 0)


def deposit(s, feat, dest, cell, code, live, arrive, fetch):
    slabs, tiles = lax.axis_size("slab"), lax.axis_size("tile")
    tile = lax.axis_index("tile")
    mine = lax.axis_index("slab") % 2
    group = slabs // 2
    attrs = feat.shape[0]
    pairs = attrs // 2
    size = CZ * YT
    tall = tiles * size
    lefts, rights = [s.left_a, s.left_b], [s.right_a, s.right_b]
    pack_particles(feat, dest, cell, code, live, s.packed, s.places)
    arrive()
    coming = [None]
    for m in range(1, group):
        device = flipped(2 * m)
        coming.append(
            [
                send(s.packed.at[0], s.packed.at[m], (s.send_p, s.recv_p), m, device),
                send(s.places.at[0], s.places.at[m], (s.send_q, s.recv_q), m, device),
            ]
        )

    fetch()

    def prepare(i):
        m, h = i // 2, i % 2
        if h == 0:
            if m:
                for copy in coming[m]:
                    copy.wait_recv()
            place_particles(m, s.places, s.spots.at[m % 2])
        build(m, h, s.packed, s.spots.at[m % 2], lefts[h], rights[h])

    def multiply(i, n):
        at = slice(2 * n * NX, (2 * n + 2) * NX)
        part = lax.dot_general(
            lefts[i % 2][...], rights[i % 2][at, :], NT, preferred_element_type=F32
        )
        if i == 0:
            s.total[:, at] = part
        else:
            s.total[:, at] += part

    def rows(which):
        return pl.ds(pl.multiple_of(which * tall, tall), tall)

    crossing, dealt = [], []

    def hand(n):
        for c in range(2):
            at = slice((2 * n + c) * NX, (2 * n + c + 1) * NX)
            s.outbox[n, c] = s.total[rows(1 - mine), at].astype(BF16)
        crossing.append(send(s.outbox.at[n], s.inbox.at[n], (s.send_c, s.recv_c), n, flipped(1)))

    def deal(n):
        crossing[n].wait_recv()
        for c in range(2):
            at = slice((2 * n + c) * NX, (2 * n + c + 1) * NX)
            total = s.total[rows(mine), at] + s.inbox[n, c].astype(F32)
            for t in range(tiles):
                s.sums[n, t, c] = total[t * size : (t + 1) * size].astype(BF16)
        dealt.append(
            [
                send(
                    s.sums.at[n, lax.rem(tile + d, tiles)],
                    s.last.at[n, d - 1],
                    (s.send_t, s.recv_t),
                    n * (tiles - 1) + d - 1,
                    ahead(d),
                )
                for d in range(1, tiles)
            ]
        )

    prepare(0)
    for i in range(2 * group):
        later = i == 1 or i % 2 == 0
        if not later and i + 1 < 2 * group:
            prepare(i + 1)
        for n in range(pairs):
            multiply(i, n)
            if i == 2 * group - 1:
                hand(n)
                if n:
                    deal(n - 1)
        if later:
            prepare(i + 1)
    deal(pairs - 1)
    s.block[...] = jnp.zeros_like(s.block)
    for n in range(pairs):
        for d in range(tiles - 1):
            dealt[n][d].wait_recv()
        for c in range(2):
            total = s.sums[n, tile, c].astype(F32)
            for d in range(tiles - 1):
                total = total + s.last[n, d, c].astype(F32)
            for z in range(CZ):
                s.block[z, :, 2 * n + c, :] = total[z * YT : (z + 1) * YT]
    for z in range(CZ):
        for y in range(YT // 2):
            s.grid[2 + z, 1 + y] = jnp.concatenate(
                [s.block[z, 2 * y], s.block[z, 2 * y + 1]], 0
            ).astype(BF16)
    return [copy for copies in coming[1:] for copy in copies] + crossing + sum(dealt, [])


def span(shift, size, width):
    if shift > 0:
        return pl.ds(size, width), pl.ds(0, width)
    if shift < 0:
        return pl.ds(width, width), pl.ds(size + width, width)
    return pl.ds(width, size), pl.ds(width, size)


def share_grid(s):
    copies = {}
    for n, (dz, dy) in enumerate(SIDES):
        from_z, to_z = span(dz, CZ, 2)
        from_y, to_y = span(dy, YT // 2, 1)
        copies[dz, dy] = send(
            s.grid.at[from_z, from_y],
            s.grid.at[to_z, to_y],
            (s.send_g, s.recv_g),
            n,
            neighbour(dz, dy),
        )
    return copies


def spread(values):
    return jnp.concatenate(
        [pltpu.roll(values, 1, 1), values, pltpu.roll(values, NX - 1, 1)], 0
    ).astype(BF16)


def cross(left, right):
    return lax.dot_general(left, right, (((0,), (0,)), ((), ())), preferred_element_type=F32)


def place(rows, columns, target_of):
    source = lax.broadcasted_iota(jnp.int32, (rows, columns), 0)
    target = lax.broadcasted_iota(jnp.int32, (rows, columns), 1)
    return jnp.where(target == target_of(source), 1.0, 0.0).astype(BF16)


def prepare_weights(s, lift_raw):
    taps = lift_raw.shape[2]
    each = taps // 3
    total = None
    for n in range(9):
        spots = place(taps, 216, lambda i: n * 24 + i // each * 8 + i % each)
        term = cross(lift_raw[n // 3, n % 3], spots)
        total = term if total is None else total + term
    s.lift[...] = total.astype(BF16)
    depth, tall = s.down_raw.shape[3:]
    for k in range(2):
        total = None
        for n in range(4):
            spots = place(depth, 4 * depth, lambda i: n * depth + i)
            term = cross(s.down_raw[n // 2, n % 2, k], spots)
            total = term if total is None else total + term
        s.down[k * tall : (k + 1) * tall] = total.astype(BF16)


def lift_level(s):
    planes, pairs = s.grid.shape[:2]
    for z in range(planes):
        for y in range(pairs):
            block = s.grid[z, y].astype(F32)
            before, after = pltpu.roll(block, 1, 1), pltpu.roll(block, NX - 1, 1)
            for p in range(2):
                at = slice(8 * p, 8 * p + 8)
                s.wide[z, 2 * y + p, 0:8] = before[at]
                s.wide[z, 2 * y + p, 8:16] = block[at]
                s.wide[z, 2 * y + p, 16:24] = after[at]
    rows = 2 * pairs - 2

    def lift_plane(z, carry):
        for y in range(0, rows, 2):
            pair = jnp.concatenate(
                [
                    jnp.concatenate(
                        [s.wide[z + a, y + p + b] for a in range(3) for b in range(3)], 0
                    ).astype(BF16)
                    for p in range(2)
                ],
                1,
            )
            values = act(dot(s.lift[...], pair))
            s.stack[z, y] = spread(values[:, :NX])
            s.stack[z, y + 1] = spread(values[:, NX:])
        return carry

    lax.fori_loop(0, planes - 2, lift_plane, 0, unroll=True)


def taps_of(weight):
    return [jnp.concatenate([weight[a, b] for a in range(3)], 0) for b in range(3)]


def conv_part(stack, lefts, acc, begun, z, j, bs):
    planes = stack.shape[0] - 2
    outs = lefts[0].shape[0] // 3
    part = None
    for b in bs:
        y = 2 * j + b
        term = dot(lefts[b], jnp.concatenate([stack[z, y], stack[z, y + 1]], 1))
        part = term if part is None else part + term
    for a in range(3):
        if 0 <= z - a < planes:
            piece = part[a * outs : (a + 1) * outs]
            if (z - a, j) in begun:
                acc[z - a, j] += piece
            else:
                acc[z - a, j] = piece
                begun.add((z - a, j))


def fine_level(s):
    lefts = taps_of(s.fine)
    source = iota(NX, 0)
    target = iota(NX, 1)
    half = NX // 2
    parity = jnp.where(target < half, 0, 1)
    sel = jnp.where(source == 2 * (target - half * parity) + parity, 1.0, 0.0).astype(BF16)
    chans = s.down.shape[0] // 2
    h = chans // 2
    lane = iota(h, 1)
    begun = set()
    copies = {}
    rows = YT // 2
    mine = lax.axis_index("slab") % 2

    def share(key, from_z, from_y, to_z, to_y, side):
        copies[key] = send(
            s.low.at[from_z, from_y],
            s.low.at[to_z, to_y],
            (s.send_l, s.recv_l),
            len(copies),
            neighbour(*side),
        )

    for js in ((0, rows - 1), (1, rows - 2)):
        for j in js:
            for z in range(CZ + 2):
                conv_part(s.stack, lefts, s.acc, begun, z, j, range(3))
            for z in range(CZ):
                values = act(s.acc[z, j]).astype(BF16)
                s.second[z, 2 * j] = values[:, :NX]
                s.second[z, 2 * j + 1] = values[:, NX:]
        for z in range(CZ // 2):
            pair = []
            for j in js:
                tall = jnp.concatenate(
                    [s.second[2 * z + a, 2 * j + b] for a in range(2) for b in range(2)], 0
                )
                pair.append(dot(tall, sel).astype(BF16))
            out = dot(s.down[...], jnp.concatenate(pair, 1))
            for p in range(2):
                q = out[:, p * NX : (p + 1) * NX]
                q00, q01, q10, q11 = (q[i * h : (i + 1) * h] for i in range(4))
                row = jnp.where(lane < half, q00, q11) + pltpu.roll(
                    jnp.where(lane < half, q01, q10), half, 1
                )
                s.low[1 + z, 1 + js[p]] = act(row).astype(BF16)
        if js[0] == 0:
            for j, dy, to in ((0, -1, rows + 1), (rows - 1, 1, 0)):
                share((0, dy), pl.ds(1, 2), 1 + j, pl.ds(1, 2), to, (0, dy))
            for j, dy, to in ((0, -1, rows + 1), (rows - 1, 1, 0)):
                share((2, dy), 1 + mine, 1 + j, 3 * (1 - mine), to, (2 * mine - 1, dy))
            for j in js:
                for dz in (-1, 1):
                    z, to_z = (1, 3) if dz < 0 else (2, 0)
                    share((dz, 0, j), z, 1 + j, to_z, 1 + j, (dz, 0))
        else:
            for dz in (-1, 1):
                z, to_z = (1, 3) if dz < 0 else (2, 0)
                at = pl.ds(2, rows - 2)
                share((dz, 0, 1), z, at, to_z, at, (dz, 0))
    return copies


def wait_some(copies, chosen):
    for key, copy in copies.items():
        if chosen(key):
            copy.wait_recv()


def pass_on(padded, s, first):
    planes, rows = padded.shape[:2]
    mine = lax.axis_index("slab") % 2
    z, to_z = planes - 2 - (planes - 3) * mine, (planes - 1) * mine
    return [
        send(padded.at[z, y], padded.at[to_z, y], (s.send_w, s.recv_w), first + i, flipped(1))
        for i, y in enumerate((0, rows - 1))
    ]


def coarse_level(s, copies):
    half = NX // 2
    chans = s.coarse.shape[2]
    outs = s.up.shape[3]
    lane = iota(chans // 2, 1)
    planes, rows = s.low.shape[:2]

    def columns(z):
        row = {r: s.low[z, r].astype(F32) for r in range(1, rows - 1)}
        turned = {r: pltpu.roll(row[r], half, 1) for r in row}
        blank = jnp.zeros_like(row[1])
        for r in (0, rows - 1):
            row[r] = turned[r] = blank
        pairs = []
        for r in range(rows - 1):
            top = jnp.where(lane < half, row[r], turned[r + 1])
            bottom = jnp.where(lane < half, turned[r], row[r + 1])
            pairs.append(jnp.concatenate([top, bottom], 0).astype(BF16))
        for b in range(3):
            s.columns[z, b] = jnp.concatenate([pairs[b], pairs[2 + b]], 1)

    def edges(z):
        low, high = (s.low[z, r].astype(F32) for r in (0, rows - 1))
        blank = jnp.zeros_like(low)
        first = [jnp.where(lane < half, v, blank) for v in (low, pltpu.roll(low, half, 1))]
        second = [jnp.where(lane < half, blank, v) for v in (pltpu.roll(high, half, 1), high)]
        return [jnp.concatenate(v, 0).astype(BF16) for v in (first, second)]

    def weights(k, taps):
        return jnp.concatenate(
            [s.coarse[a, b, :, k * chans : (k + 1) * chans] for a, b in taps], 1
        )

    def product(z, k, taps):
        return dot(
            weights(k, taps), jnp.concatenate([s.columns[z + a, b] for a, b in taps], 0)
        )

    for z in (1, 2):
        columns(z)
    for z, at in ((0, (1, 2)), (1, (0, 1))):
        for k in range(3):
            s.part[z, k] = product(z, k, [(a, b) for a in at for b in range(3)])
    for key, copy in copies.items():
        if key[1] == 0:
            copy.wait_recv()
    for z in (0, 3):
        columns(z)
    for z, a in ((0, 0), (1, 2)):
        for k in range(3):
            s.part[z, k] += product(z, k, [(a, b) for b in range(3)])
    wait_some(copies, lambda key: key[0] == 0)
    passed = pass_on(s.low, s, 0)
    wait_some(copies, lambda key: key[0] == 2)
    for copy in passed:
        copy.wait_recv()
    edge = [edges(z) for z in range(planes)]
    outer = jnp.concatenate(
        [
            jnp.concatenate([edge[a][i], edge[a + 1][i]], 1)
            for a in range(3)
            for i in range(2)
        ],
        0,
    )
    halos = [dot(weights(k, [(a, b) for a in range(3) for b in (0, 2)]), outer) for k in range(3)]

    source = lax.broadcasted_iota(jnp.int32, (NX, 4 * NX), 0)
    target = lax.broadcasted_iota(jnp.int32, (NX, 4 * NX), 1)
    spot = target % NX
    want = target // (2 * NX) * half + spot // 2
    sel = jnp.where((source == want) & (spot % 2 == target // NX % 2), 1.0, 0.0).astype(BF16)
    lane = iota(chans, 1)
    lefts = [
        jnp.concatenate([s.up[a, b, k] for a in range(2) for b in range(2)], 0) for k in range(2)
    ]
    onward = {}
    mine = lax.axis_index("slab") % 2

    def share(key, from_z, from_y, to_z, to_y, side):
        onward[key] = send(
            s.joined.at[from_z, from_y],
            s.joined.at[to_z, to_y],
            (s.send_j, s.recv_j),
            len(onward),
            neighbour(*side),
        )

    for z in range(planes - 2):
        for j in range(2):
            at = slice(j * NX, (j + 1) * NX)
            own = lane < half if j == 0 else lane >= half
            before, same, after = (
                s.part[z, k, :, at]
                + jnp.where(own, halos[k][:, z * NX : (z + 1) * NX], 0.0)
                for k in range(3)
            )
            before = jnp.where(
                lane % half == 0, pltpu.roll(before, half + 1, 1), pltpu.roll(before, 1, 1)
            )
            after = jnp.where(
                lane % half == half - 1,
                pltpu.roll(after, half - 1, 1),
                pltpu.roll(after, NX - 1, 1),
            )
            coarse = act(before + same + after).astype(BF16)
            wide = dot(coarse, sel).astype(BF16)
            right = [
                jnp.concatenate(
                    [wide[:, k * NX : (k + 1) * NX], wide[:, (2 + k) * NX : (3 + k) * NX]], 1
                )
                for k in range(2)
            ]
            raised = dot(lefts[0], right[0]) + dot(lefts[1], right[1])
            for a in range(2):
                for b in range(2):
                    for p in range(2):
                        y = 2 * (2 * j + p) + b
                        piece = raised[
                            (2 * a + b) * outs : (2 * a + b + 1) * outs, p * NX : (p + 1) * NX
                        ]
                        s.joined[1 + 2 * z + a, 1 + y] = (
                            s.second[2 * z + a, y].astype(F32) + piece
                        ).astype(BF16)
            dy, edge, to = ((-1, 1, YT + 1), (1, YT, 0))[j]
            dz, face, to_z = ((-1, 1, CZ + 1), (1, CZ, 0))[z]
            both = pl.ds(1 + 2 * z, 2)
            share((0, dy, z), both, edge, both, to, (0, dy))
            if z:
                away = 5 * (1 - mine)
                share((2, dy), 1 + 3 * mine, edge, away, to, (2 * mine - 1, dy))
            across = pl.ds(1 + 4 * j, 4)
            share((dz, 0, j), face, across, to_z, across, (dz, 0))
    return onward, passed


def merge_level(s, copies, head, out):
    lefts = taps_of(s.merge)
    begun = set()
    last = YT // 2 - 1

    def widen(z, y):
        s.stack[z, y] = spread(s.joined[z, y].astype(F32))

    def inner(j):
        return [b for b in range(3) if (j, b) != (0, 0) and (j, b) != (last, 2)]

    for z in range(1, CZ + 1):
        for y in range(1, YT + 1):
            widen(z, y)
    for z in range(1, CZ + 1):
        for j in range(last + 1):
            conv_part(s.stack, lefts, s.acc, begun, z, j, inner(j))
    for key, copy in copies.items():
        if key[1] == 0:
            copy.wait_recv()
    for z in (0, CZ + 1):
        for y in range(1, YT + 1):
            widen(z, y)
        for j in range(last + 1):
            conv_part(s.stack, lefts, s.acc, begun, z, j, inner(j))
    wait_some(copies, lambda key: key[0] == 0)
    passed = pass_on(s.joined, s, 2)

    def outer(planes):
        for z in planes:
            for y in (0, YT + 1):
                widen(z, y)
            for j, b in ((0, 0), (last, 2)):
                conv_part(s.stack, lefts, s.acc, begun, z, j, [b])

    outer(range(1, CZ + 1))
    wait_some(copies, lambda key: key[0] == 2)
    for copy in passed:
        copy.wait_recv()
    outer((0, CZ + 1))
    for z in range(CZ):
        for j in range(last + 1):
            moved = dot(head[...], act(s.acc[z, j]).astype(BF16))
            for p in range(2):
                out[:, z, 2 * j + p, :] = moved[: out.shape[0], p * NX : (p + 1) * NX]
    return passed


FAR = ("fine", "down_raw", "coarse", "up", "merge")


def step_kernel(names, feat, dest, cell, code, live, lift_raw, head, *rest):
    far, out, scratch = rest[: len(FAR)], rest[len(FAR)], rest[len(FAR) + 1 :]
    s = types.SimpleNamespace(**dict(zip(names, scratch, strict=True)))
    slabs, tiles = lax.axis_size("slab"), lax.axis_size("tile")
    devices = [flipped(1)] + [flipped(2 * m) for m in range(1, slabs // 2)]
    devices += [ahead(d) for d in range(1, tiles)] + [neighbour(dz, dy) for dz, dy in SIDES]
    barrier = pltpu.get_barrier_semaphore()
    for device in devices:
        pl.semaphore_signal(barrier, inc=1, device_id=device, device_id_type=MESH)
    fetches = {}
    for n, name in enumerate(FAR):
        fetches[name] = pltpu.make_async_copy(far[n], getattr(s, name), s.fetched.at[n])

    def arrive():
        pl.semaphore_wait(barrier, len(devices))

    def fetch():
        for copy in fetches.values():
            copy.start()

    sent = deposit(s, feat, dest, cell, code, live, arrive, fetch)
    grids = share_grid(s)
    fetches["down_raw"].wait()
    prepare_weights(s, lift_raw)
    for copy in grids.values():
        copy.wait_recv()
    lift_level(s)
    fetches["fine"].wait()
    lows = fine_level(s)
    fetches["coarse"].wait()
    fetches["up"].wait()
    joins, passed = coarse_level(s, lows)
    fetches["merge"].wait()
    passed = passed + merge_level(s, joins, head, out)
    for copy in sent + passed + list(grids.values()) + list(lows.values()) + list(joins.values()):
        copy.wait_send()


def step(features, destination, cells, codes, live, lift, fine, down, coarse, up, merge, head):
    attrs, total = features.shape
    slabs, tiles = lax.axis_size("slab"), lax.axis_size("tile")
    size = CZ * YT
    group = slabs // 2
    pairs = attrs // 2
    outs, chans = fine.shape[2], coarse.shape[2]
    planes, rows = CZ + 2, YT + 2
    down = down.swapaxes(3, 4)

    def sems(count):
        return pltpu.SemaphoreType.DMA((count,))

    scratch = dict(
        packed=pltpu.VMEM((group, 16, total // 2), BF16),
        places=pltpu.VMEM((group, total // LANES, LANES), jnp.int32),
        spots=pltpu.VMEM((2, 2, total // LANES, LANES), F32),
        left_a=pltpu.VMEM((2 * tiles * size, total // 2), BF16),
        left_b=pltpu.VMEM((2 * tiles * size, total // 2), BF16),
        right_a=pltpu.VMEM((attrs * NX, total // 2), BF16),
        right_b=pltpu.VMEM((attrs * NX, total // 2), BF16),
        total=pltpu.VMEM((2 * tiles * size, attrs * NX), F32),
        outbox=pltpu.VMEM((pairs, 2, tiles * size, NX), BF16),
        inbox=pltpu.VMEM((pairs, 2, tiles * size, NX), BF16),
        sums=pltpu.VMEM((pairs, tiles, 2, size, NX), BF16),
        last=pltpu.VMEM((pairs, tiles - 1, 2, size, NX), BF16),
        block=pltpu.VMEM((CZ, YT, 8, NX), F32),
        grid=pltpu.VMEM((CZ + 4, YT // 2 + 2, 16, NX), BF16),
        wide=pltpu.VMEM((CZ + 4, YT + 4, 24, NX), F32),
        lift=pltpu.VMEM((outs, 216), BF16),
        down=pltpu.VMEM((2 * chans, 4 * outs), BF16),
        stack=pltpu.VMEM((planes, rows, 3 * outs, NX), BF16),
        acc=pltpu.VMEM((CZ, YT // 2, outs, 2 * NX), F32),
        second=pltpu.VMEM((CZ, YT, outs, NX), BF16),
        low=pltpu.VMEM((CZ // 2 + 2, YT // 2 + 2, chans // 2, NX), BF16),
        columns=pltpu.VMEM((CZ // 2 + 2, 3, chans, 2 * NX), BF16),
        part=pltpu.VMEM((CZ // 2, 3, chans, 2 * NX), F32),
        joined=pltpu.VMEM((planes, rows, outs, NX), BF16),
        fine=pltpu.VMEM(fine.shape, BF16),
        down_raw=pltpu.VMEM(down.shape, BF16),
        coarse=pltpu.VMEM(coarse.shape, BF16),
        up=pltpu.VMEM(up.shape, BF16),
        merge=pltpu.VMEM(merge.shape, BF16),
        fetched=sems(len(FAR)),
    )
    for name, count in dict(
        p=group, q=group, c=pairs, t=pairs * (tiles - 1), g=8, l=10, j=10, w=4
    ).items():
        scratch["send_" + name] = sems(count)
        scratch["recv_" + name] = sems(count)
    near = pl.BlockSpec(memory_space=pltpu.VMEM)
    far = pl.BlockSpec(memory_space=pl.ANY)

    def kernel(*refs):
        step_kernel(list(scratch), *refs)

    return pl.pallas_call(
        kernel,
        in_specs=[near] * 7 + [far] * 5,
        out_specs=near,
        out_shape=jax.ShapeDtypeStruct((head.shape[0], CZ, YT, NX), F32),
        scratch_shapes=list(scratch.values()),
        compiler_params=pltpu.CompilerParams(
            collective_id=0, has_side_effects=True, vmem_limit_bytes=60 << 20
        ),
        name="step",
    )(
        features,
        destination.reshape(-1, LANES),
        cells.reshape(-1, LANES),
        codes.reshape(-1, LANES),
        live.reshape(1, 1),
        lift.swapaxes(2, 3),
        head,
        fine,
        down,
        coarse,
        up,
        merge,
    )


def solution(mesh):
    split = P(("slab", "tile"))
    placed = (P(None, ("slab", "tile")), P(("slab", "tile"), None)) + (split,) * 3 + (P(),) * 7
    return jax.shard_map(
        step, mesh=mesh, in_specs=placed, out_specs=P(None, "slab", "tile", None), check_vma=False
    )
```
